32 devices in a mesh: op: 4 (over y, core), tm: 8 (over z, x).
Axes of the slice: x: 2, y: 2, z: 4, core: 2. Of those that a mesh axis runs over, the one named last changes fastest.
Arguments:
- mesons: float32 [4, 16, 2, 384, 384], P('op', 'tm'), may hold values from -6 to 6
- perambulator: float32 [16, 2, 384, 384], P('tm', None, 'op'), may hold values from -0.21875 to 0.21875
- graph_list: int32 [32, 4], P('op'), may hold values from -2 to 7, as said below
Outputs:
- diagrams: float32 [384, 6144], P('op', 'tm')
The draws below stay inside these ranges and needn't reach their ends.
Inputs may be any that keep to these rules, and one draw needn't show every extreme that they name: `graph_list`: each row is a product slot of the op index that holds it: first operator id and second operator id (0 to 3, the second taken at the sink time), diagram id (0 to 7) and an integer weight. Weight 0 marks an empty slot; live weights are -2, -1, 1 or 2 and the live slots of an op index come first. In every draw some op index has all 8 slots live.
All inputs are finite; a program needn't handle non-finite values.
Results may differ from the reference program's by a relative error of at most 0.0003.
Values sent between devices are 32-bit elements; how exact they have to be, the bound alone decides.
No kernel may reach another device: no remote copies, remote signals or barrier semaphores. Data moves between devices by JAX's collectives and lax.ppermute only.
A program may use at most 128 MiB of HBM per device.

```python
import jax
import jax.numpy as jnp
from jax import lax

N = 384
TT_DEV = 2
PSLOT = 8
DIAG = 8
OPS = 4
TIMES = 16
N_OP = 4


def draw_graph_list(key, part):
    subkeys = jax.random.split(key, 7)
    total_slots = N_OP * PSLOT
    slot_index = jnp.arange(total_slots, dtype=jnp.int32) % PSLOT
    device_index = jnp.arange(total_slots, dtype=jnp.int32) // PSLOT
    counts = jax.random.randint(subkeys[0], (N_OP,), 1, PSLOT // 2 + 1)
    busiest = jax.random.randint(subkeys[1], (), 0, N_OP)
    counts = jnp.where(jnp.arange(N_OP, dtype=jnp.int32) == busiest, PSLOT, counts)
    first_operand = jax.random.randint(subkeys[2], (total_slots,), 0, OPS)
    second_operand = jax.random.randint(subkeys[3], (total_slots,), 0, OPS)
    offsets = jax.random.randint(subkeys[4], (), 0, DIAG)
    random_diagram = jax.random.randint(subkeys[5], (total_slots,), 0, DIAG)
    diagram = jnp.where(device_index == busiest, (slot_index + offsets) % DIAG, random_diagram)
    level = jax.random.randint(subkeys[6], (total_slots,), 0, 4)
    weight = level - 2 + (level >= 2).astype(jnp.int32)
    weight = jnp.where(slot_index < counts[device_index], weight, 0)
    return jnp.stack([first_operand, second_operand, diagram, weight], axis=1).astype(jnp.int32)


def block_levels(own_key, dims, pieces, low, top_value):
    factor_of = 1.0
    for axis_at, shards_of in pieces:
        heights = jax.random.uniform(jax.random.fold_in(jax.random.fold_in(own_key, 6), axis_at), (shards_of,), jnp.float32, low / len(pieces), top_value / len(pieces))
        factor_of = factor_of * jnp.repeat(jnp.exp(heights), dims[axis_at] // shards_of).reshape((-1,) + (1,) * (len(dims) - 1 - axis_at))
    return factor_of


def centred(key, shape, spread, reach, cuts=(), held_as=jnp.bfloat16):
    drawn = spread * jax.random.normal(key, shape, jnp.float32)
    if cuts:
        drawn = drawn * block_levels(key, shape, cuts, -0.22, 0.18)
    return jnp.clip(drawn, -reach, reach).astype(held_as)


def setup_inputs(seed: int = 0) -> dict:
    splits = jax.random.split(jax.random.key(seed), 4)
    return {
        "mesons": centred(splits[0], (OPS, TIMES, 2, N, N), 1.0, 6.0, ((0, 4), (1, 8)), jnp.float32),
        "perambulator": centred(splits[1], (TIMES, 2, N, N), (2 * N) ** -0.5, 0.21875, ((0, 8), (2, 4)), jnp.float32),
        "graph_list": draw_graph_list(jax.random.fold_in(splits[3], 71), 0),
    }


HIGHEST = lax.Precision.HIGHEST


def matmul_high(first, second):
    return jnp.matmul(first, second, precision=HIGHEST)


def complex_product(first, second):
    first_real = first[..., 0, :, :]
    first_imag = first[..., 1, :, :]
    second_real = second[..., 0, :, :]
    second_imag = second[..., 1, :, :]
    real_part = matmul_high(first_real, second_real) - matmul_high(first_imag, second_imag)
    imag_part = matmul_high(first_real, second_imag) + matmul_high(first_imag, second_real)
    return jnp.stack([real_part, imag_part], axis=-3)


def adjoint(matrix):
    swapped = jnp.swapaxes(matrix, -1, -2)
    return jnp.stack([swapped[..., 0, :, :], -swapped[..., 1, :, :]], axis=-3)


def dress(mesons, tau):
    return complex_product(adjoint(tau), complex_product(mesons, tau))


def reference(mesons, perambulator, graph_list):
    times_all = mesons.shape[1]

    def dress_time(time_index):
        return dress(mesons[:, time_index], perambulator[time_index][None])

    dressed = lax.map(dress_time, jnp.arange(times_all, dtype=jnp.int32))
    factor = (2.0 * N) ** -0.5 / times_all

    def over_times(totals, time_index):
        later_index = (time_index + TT_DEV) % times_all
        current = dressed[time_index]
        sink_side = dressed[later_index]

        def over_entries(totals, entry):
            def include(totals):
                product = complex_product(current[entry[0]], sink_side[entry[1]])
                previous = totals[entry[2]]
                return totals.at[entry[2]].set(previous + (entry[3].astype(jnp.float32) * factor) * product)

            return lax.cond(entry[3] != 0, include, lambda unchanged: unchanged, totals), None

        totals, _ = lax.scan(over_entries, totals, graph_list)
        return totals, None

    totals = jnp.zeros((DIAG, 2, N, N), jnp.float32)
    totals, _ = lax.scan(over_times, totals, jnp.arange(times_all, dtype=jnp.int32))
    return jnp.transpose(totals, (2, 0, 1, 3)).reshape(N, DIAG * 2 * N)
```

```python
import functools

import jax
import jax.numpy as jnp
from jax import lax
from jax.experimental import pallas as pl
from jax.experimental.pallas import tpu as pltpu
from jax.sharding import PartitionSpec as P

DIAG = 8
PARTS = 2
LANES = 128


VMEM = pl.BlockSpec(memory_space=pltpu.VMEM)
SMEM = pl.BlockSpec(memory_space=pltpu.SMEM)


def exchanged(array, axis, mask):
    size = lax.axis_size(axis)
    return lax.ppermute(array, axis, [(i, i ^ mask) for i in range(size)])


def shifted(array, axis, by):
    size = lax.axis_size(axis)
    return lax.ppermute(array, axis, [(i, (i + by) % size) for i in range(size)])


def two_terms(value):
    high = value.astype(jnp.bfloat16)
    low = (value - high.astype(jnp.float32)).astype(jnp.bfloat16)
    return high, low


def store_terms(refs, rows, columns, value):
    high, low = two_terms(value)
    refs[0][rows, columns] = high
    refs[1][rows, columns] = low


def product(first, second):
    dot = functools.partial(jnp.dot, preferred_element_type=jnp.float32)
    return dot(first[0], second[0]) + (dot(first[0], second[1]) + dot(first[1], second[0]))


def dress_kernel(op_count, place_ref, mesons_ref, *refs):
    tau_refs = refs[:op_count]
    row_refs = refs[op_count : 2 * op_count]
    chunk_refs = refs[2 * op_count : -8]
    tau, dressed, meson_h, meson_l, right_h, right_l, left_h, left_l = refs[-8:]
    size = tau.shape[1]
    rows = size // op_count
    me = place_ref[0]
    for mask in range(op_count):
        start = pl.multiple_of((me ^ mask) * rows, rows)
        tau[:, pl.ds(start, rows), :] = tau_refs[mask][...]
    low, high = pl.ds(0, size), pl.ds(size, size)
    every = pl.ds(0, size)
    right = (right_h, right_l)
    store_terms((meson_h, meson_l), every, low, mesons_ref[0, 0, 0])
    store_terms((meson_h, meson_l), every, high, mesons_ref[0, 0, 1])
    tau_real, tau_imag = tau[0], tau[1]
    store_terms(right, low, low, tau_real)
    store_terms(right, high, high, tau_real)
    store_terms(right, low, high, tau_imag)
    store_terms(right, high, low, -tau_imag)
    store_terms((left_h, left_l), every, low, tau_real.T)
    store_terms((left_h, left_l), every, high, tau_imag.T)
    half = product((meson_h[...], meson_l[...]), (right_h[...], right_l[...]))
    half_real, half_imag = half[:, :size], half[:, size:]
    store_terms(right, low, low, half_real)
    store_terms(right, low, high, half_imag)
    store_terms(right, high, low, half_imag)
    store_terms(right, high, high, -half_real)
    full = product((left_h[...], left_l[...]), (right_h[...], right_l[...]))
    dressed[0] = full[:, :size]
    dressed[1] = full[:, size:]
    for mask in range(op_count):
        start = pl.multiple_of((me ^ mask) * rows, rows)
        row_refs[mask][...] = dressed[:, pl.ds(start, rows), :]
    for chunk, ref in enumerate(chunk_refs):
        ref[...] = dressed[:, :, chunk * LANES : (chunk + 1) * LANES]


def dress(place, mesons, time, tau_pieces):
    op_count = len(tau_pieces)
    rows, size = tau_pieces[0].shape[1:]
    chunks = size // LANES
    bf16, f32 = jnp.bfloat16, jnp.float32
    outs = [jax.ShapeDtypeStruct((PARTS, rows, size), f32)] * op_count + [
        jax.ShapeDtypeStruct((PARTS, size, LANES), f32)
    ] * chunks
    wide = pltpu.VMEM((size, PARTS * size), bf16)
    block = pltpu.VMEM((PARTS * size, PARTS * size), bf16)
    whole = pltpu.VMEM((PARTS, size, size), f32)
    results = pl.pallas_call(
        functools.partial(dress_kernel, op_count),
        out_shape=outs,
        grid=(1,),
        in_specs=[
            SMEM,
            pl.BlockSpec((1, 1, PARTS, size, size), lambda i: (0, time, 0, 0, 0)),
        ]
        + [VMEM] * op_count,
        out_specs=[VMEM] * len(outs),
        scratch_shapes=[whole, whole, wide, wide, block, block, wide, wide],
        cost_estimate=pl.CostEstimate(
            flops=3 * 16 * size**3, bytes_accessed=20 * PARTS * size * size, transcendentals=0
        ),
        name=f"dress_{time}",
    )(place, mesons, *tau_pieces)
    return results[:op_count], results[op_count:]


def contract_kernel(op_count, times, nx, nz, factor, place_ref, slots_ref, *refs):
    count = op_count * times
    first_refs, second_refs = refs[:count], refs[count : 2 * count]
    out_refs = refs[2 * count : 2 * count + nx]
    left_h, left_l, right_h, right_l, products, totals = refs[2 * count + nx :]
    rows, size = first_refs[0].shape[1:]
    me, z, x = place_ref[0], place_ref[1], place_ref[2]
    for mask in range(op_count):
        for time in range(times):
            for part in range(PARTS):
                store_terms(
                    (left_h, left_l),
                    pl.ds(mask * rows, rows),
                    pl.ds((time * PARTS + part) * size, size),
                    first_refs[mask * times + time][part],
                )
    for mask in range(op_count):
        for time in range(times):
            ref = second_refs[mask * times + time]
            real, imag = ref[0], ref[1]
            above = pl.ds(time * PARTS * size, size)
            below = pl.ds((time * PARTS + 1) * size, size)
            west, east = pl.ds(0, LANES), pl.ds(LANES, LANES)
            store_terms((right_h, right_l), above, west, real)
            store_terms((right_h, right_l), above, east, imag)
            store_terms((right_h, right_l), below, west, -imag)
            store_terms((right_h, right_l), below, east, real)
        result = product((left_h[...], left_l[...]), (right_h[...], right_l[...]))
        for part in range(PARTS):
            products[mask, part] = result[:, part * LANES : (part + 1) * LANES].reshape(
                op_count, rows, LANES
            )
    totals[...] = jnp.zeros_like(totals)

    def add_slot(slot, carry):
        first = slots_ref[slot, 0] ^ me
        second = slots_ref[slot, 1] ^ me
        diagram = slots_ref[slot, 2]
        weight = slots_ref[slot, 3]

        @pl.when(weight != 0)
        def _():
            scale = weight.astype(jnp.float32) * factor
            for part in range(PARTS):
                totals[diagram * PARTS + part] += scale * products[second, part, first]

        return carry

    lax.fori_loop(0, slots_ref.shape[0], add_slot, 0)
    blocks = totals.shape[0] // (nx * nz)
    for xmask in range(nx):
        for zmask in range(nz):
            start = ((z ^ zmask) * nx + (x ^ xmask)) * blocks
            for block in range(blocks):
                out_refs[xmask][zmask, block] = totals[start + block]


def contract(place, slots, firsts, seconds, nx, nz, factor):
    op_count, times = len(firsts), len(firsts[0])
    rows, size = firsts[0][0].shape[1:]
    bf16, f32 = jnp.bfloat16, jnp.float32
    blocks = DIAG * PARTS // (nx * nz)
    depth = times * PARTS * size
    flat = [array for group in firsts for array in group]
    flat += [array for group in seconds for array in group]
    return pl.pallas_call(
        functools.partial(contract_kernel, op_count, times, nx, nz, factor),
        out_shape=[jax.ShapeDtypeStruct((nz, blocks, rows, LANES), f32)] * nx,
        in_specs=[SMEM, SMEM] + [VMEM] * len(flat),
        out_specs=[VMEM] * nx,
        scratch_shapes=[
            pltpu.VMEM((op_count * rows, depth), bf16),
            pltpu.VMEM((op_count * rows, depth), bf16),
            pltpu.VMEM((depth, PARTS * LANES), bf16),
            pltpu.VMEM((depth, PARTS * LANES), bf16),
            pltpu.VMEM((op_count, PARTS, op_count, rows, LANES), f32),
            pltpu.VMEM((DIAG * PARTS, rows, LANES), f32),
        ],
        cost_estimate=pl.CostEstimate(
            flops=6 * op_count * rows * depth * op_count * PARTS * LANES,
            bytes_accessed=4 * sum(a.size for a in flat),
            transcendentals=0,
        ),
        name="contract",
    )(place, slots, *flat)


def add_kernel(count, *refs):
    ins, outs = refs[:count], refs[count:]
    for index, out in enumerate(outs):
        total = ins[0][index]
        for ref in ins[1:]:
            total = total + ref[index]
        out[...] = total


def add_groups(arrays):
    depth, *inner = arrays[0].shape
    return pl.pallas_call(
        functools.partial(add_kernel, len(arrays)),
        out_shape=[jax.ShapeDtypeStruct(tuple(inner), jnp.float32)] * depth,
        in_specs=[VMEM] * len(arrays),
        out_specs=[VMEM] * depth,
        cost_estimate=pl.CostEstimate(
            flops=arrays[0].size, bytes_accessed=8 * len(arrays) * arrays[0].size, transcendentals=0
        ),
        name="add_groups",
    )(*arrays)


def join_kernel(chunks, *refs):
    ins, out = refs[:-1], refs[-1]
    terms = len(ins) // chunks
    blocks = ins[0].shape[0]
    for block in range(blocks):
        for chunk in range(chunks):
            total = ins[chunk * terms][block]
            for ref in ins[chunk * terms + 1 : (chunk + 1) * terms]:
                total = total + ref[block]
            start = (block * chunks + chunk) * LANES
            out[:, start : start + LANES] = total


def join(groups):
    blocks, rows, width = groups[0][0].shape
    flat = [array for group in groups for array in group]
    return pl.pallas_call(
        functools.partial(join_kernel, len(groups)),
        out_shape=jax.ShapeDtypeStruct((rows, blocks * len(groups) * width), jnp.float32),
        in_specs=[VMEM] * len(flat),
        out_specs=VMEM,
        name="join",
    )(*flat)


def gathered(array):
    op_count = lax.axis_size("op")
    pieces = [None] * op_count
    for mask in range(0, op_count, 2):
        pieces[mask] = array if mask == 0 else exchanged(array, "op", mask)
    for mask in range(0, op_count, 2):
        pieces[mask + 1] = exchanged(pieces[mask], "op", 1)
    return pieces


def local(mesons, perambulator, graph_list):
    times = mesons.shape[1]
    size = mesons.shape[-1]
    chunks = size // LANES
    op_count, tm_count = lax.axis_size("op"), lax.axis_size("tm")
    nx = 1 << ((tm_count.bit_length() - 1) // 2)
    nz = tm_count // nx
    factor = (2.0 * size) ** -0.5 / (times * tm_count)
    tm_index = lax.axis_index("tm")
    place = jnp.stack([lax.axis_index("op"), tm_index // nx, tm_index % nx]).astype(jnp.int32)

    taus = [gathered(perambulator[time]) for time in range(times)]
    slots = graph_list
    for bit in reversed(range(op_count.bit_length() - 1)):
        slots = jnp.concatenate([slots, exchanged(slots, "op", 1 << bit)])

    firsts = [[None] * times for _ in range(op_count)]
    columns = [None] * times
    for time in range(times):
        rows_of, columns[time] = dress(place, mesons, time, taus[time])
        for mask in range(op_count):
            piece = rows_of[mask]
            firsts[mask][time] = piece if mask == 0 else exchanged(piece, "op", mask)

    sinks = [[shifted(columns[time][chunk], "tm", -1) for time in range(times)] for chunk in range(chunks)]
    groups = []
    for chunk in range(chunks):
        per_time = [gathered(sinks[chunk][time]) for time in range(times)]
        seconds = [[per_time[time][mask] for time in range(times)] for mask in range(op_count)]
        parts = contract(place, slots, firsts, seconds, nx, nz, factor)
        received = [parts[0]] + [exchanged(parts[mask], "tm", mask) for mask in range(1, nx)]
        summed = add_groups(received)
        groups.append(
            [summed[0]] + [exchanged(summed[mask], "tm", mask * nx) for mask in range(1, nz)]
        )
    return join(groups)


def solution(mesh):
    placed = (P("op", "tm", None, None, None), P("tm", None, "op", None), P("op", None))
    return jax.shard_map(
        local, mesh=mesh, in_specs=placed, out_specs=P("op", "tm"), check_vma=False
    )
```
